256 devices in a mesh: pipe: 8 (over z_hi, y), row: 8 (over z_lo, core), col: 4 (over x).
Axes of the slice: x: 4, y: 4, z: 8 (z_hi: 2, z_lo: 4; z = z_hi * 4 + z_lo), core: 2. Of those that a mesh axis runs over, the one named last changes fastest.
Arguments:
- tokens: bfloat16 [8, 256, 4096], P('pipe', 'row', 'col'), may hold values from -12 to 12
- norm_gain: float32 [8, 4096], P('pipe', 'col'), may hold values from 0.5 to 2
- gate_weight: bfloat16 [8, 4096, 14336], P('pipe', 'col', 'row'), may hold values from -0.09375 to 0.09375
- up_weight: bfloat16 [8, 4096, 14336], P('pipe', 'col', 'row'), may hold values from -0.09375 to 0.09375
- down_weight: bfloat16 [8, 14336, 4096], P('pipe', ('row', 'col')), may hold values from -0.046875 to 0.046875
Outputs:
- handed: bfloat16 [8, 256, 4096], P('pipe', 'row', 'col')
The draws below stay inside these ranges and needn't reach their ends.
All inputs are finite; a program needn't handle non-finite values.
Results may differ from the reference program's by a relative error of at most 0.024.
Values may be sent and summed in bfloat16 or wider, within the bound.
A program may use at most 64 MiB of HBM per device.

```python
import math
import jax
import jax.numpy as jnp
from jax import lax

D = 4096
FF = 14336
TOKENS = 256
SECTIONS = 8
N_ROW = 8
N_COL = 4


def draw_tokens(key, part):
    key_base, key_jitter, key_rows = jax.random.split(key, 3)
    column = jnp.arange(D, dtype=jnp.float32)
    rising = jnp.sqrt(1.0 + 2.0 * column / max(D - 1, 1))
    jitter = jnp.exp(jax.random.uniform(key_jitter, (SECTIONS, 1, D), jnp.float32, -0.5, 0.5))
    row_scale = jnp.exp(jax.random.uniform(key_rows, (SECTIONS, TOKENS, 1), jnp.float32, math.log(0.1), 0.0))
    base = jnp.clip(jax.random.normal(key_base, (SECTIONS, TOKENS, D), jnp.float32), -4.0, 4.0)
    return (base * rising * jitter * row_scale).astype(jnp.bfloat16)


def steps_of(stream_key, dims, cuts, low, top_value):
    def one(dim, blocks):
        heights = jax.random.uniform(jax.random.fold_in(jax.random.fold_in(stream_key, 6), dim), (blocks,), jnp.float32, low / len(cuts), top_value / len(cuts))
        return jnp.repeat(jnp.exp(heights), dims[dim] // blocks).reshape((-1,) + (1,) * (len(dims) - dim - 1))

    level = one(*cuts[0])
    for cut in cuts[1:]:
        level = level * one(*cut)
    return level


def gaussian(own_key, extent, width, limit, cuts=(), kind=jnp.bfloat16):
    array = width * jax.random.normal(own_key, extent, jnp.float32)
    if cuts:
        array = array * steps_of(own_key, extent, cuts, -0.22, 0.18)
    return jnp.clip(array, -limit, limit).astype(kind)


def setup_inputs(seed: int = 0) -> dict:
    keys = jax.random.split(jax.random.key(seed), 6)
    return {
        "tokens": draw_tokens(jax.random.fold_in(keys[5], 71), 0),
        "norm_gain": jnp.clip(jnp.exp(math.log(2.0) - 1.3862944 * jax.random.uniform(keys[1], (SECTIONS, D), jnp.float32) ** steps_of(keys[1], (SECTIONS, D), ((0, 8), (1, 4)), -0.2, 0.2)), 0.5, 2.0),
        "gate_weight": gaussian(keys[2], (SECTIONS, D, FF), D ** -0.5, 0.09375, ((0, 8), (1, 4), (2, 8))),
        "up_weight": gaussian(keys[3], (SECTIONS, D, FF), D ** -0.5, 0.09375, ((0, 8), (1, 4), (2, 8))),
        "down_weight": gaussian(keys[4], (SECTIONS, FF, D), FF ** -0.5, 0.046875, ((0, 8), (1, 32))),
    }


EPS = 1e-05

def reference(tokens, norm_gain, gate_weight, up_weight, down_weight):
    pieces = N_ROW * N_COL
    block_width = FF // pieces

    def one_section(section_args):
        inputs, gain, gate_w, up_w, down_w = section_args
        widened = inputs.astype(jnp.float32)
        mean_square = lax.optimization_barrier(jnp.mean(widened * widened, axis=1, keepdims=True))
        normed = (widened * lax.rsqrt(mean_square + EPS) * gain.astype(jnp.float32)[None, :]).astype(jnp.bfloat16)
        gate_value = jnp.dot(normed, gate_w, preferred_element_type=jnp.float32)
        up_value = jnp.dot(normed, up_w, preferred_element_type=jnp.float32)
        hidden = (jax.nn.silu(gate_value) * up_value).astype(jnp.bfloat16)
        hidden_blocks = hidden.reshape(TOKENS, pieces, block_width).transpose(1, 0, 2)
        down_blocks = down_w.reshape(pieces, block_width, D)

        def add_block(total, pair):
            hidden_part, weight_part = pair
            rounded = jnp.dot(hidden_part, weight_part, preferred_element_type=jnp.float32).astype(jnp.bfloat16)
            rounded = lax.optimization_barrier(rounded)
            return (total + rounded.astype(jnp.float32), None)
        total, _ = lax.scan(add_block, jnp.zeros((TOKENS, D), jnp.float32), (hidden_blocks, down_blocks))
        branch_out = total.astype(jnp.bfloat16)
        return (widened + branch_out.astype(jnp.float32)).astype(jnp.bfloat16)
    layer_out = lax.map(one_section, (tokens, norm_gain, gate_weight, up_weight, down_weight))
    return jnp.roll(layer_out, 1, axis=0)
```

```python
import functools

import jax
import jax.numpy as jnp
from jax import lax
from jax.experimental import pallas as pl
from jax.experimental.pallas import tpu as pltpu
from jax.sharding import PartitionSpec as P

D = 4096
EPS = 1e-05
MESH = pl.DeviceIdType.MESH
F32 = jnp.float32
BF16 = jnp.bfloat16

ORDER = (0, 2, 3, 1)
OPP, RIGHT, LEFT, OWN = 0, 1, 2, 3

KINDS = (
    "tok", "fwd", "ss_r", "ss_l", "ss_o",
    "m1r", "m1l", "m3r", "m3l", "m2r", "m2l",
    "ex0", "ex1", "ex2", "ex3",
    "n1r", "n1l", "n3r", "n3l", "n2r", "n2l",
    "zr", "hand",
)
NK = len(KINDS)


def kernel(
    tok_ref, gain_ref, gate_hbm, up_hbm, down_hbm, out_ref,
    w, wd, xs, ssend, srecv,
    p1, d3, q, m2, own, r1, r3, r2,
    hid, ps, pr, po, n1, n3, n2, nq, t1, t3, t2,
    racc, zsend, zrecv, hsend,
    send_sem, recv_sem, w_sem,
):
    pipe, row, x = lax.axis_index("pipe"), lax.axis_index("row"), lax.axis_index("col")
    z, core = row // 2, row % 2
    zx = {1: z + 1 - 2 * (z % 2), 2: z + 2 - 4 * (z // 2), 3: 3 - z}

    partner = (pipe, 2 * z + 1 - core, x)
    zpeer = {e: (pipe, 2 * zx[e] + core, x) for e in (1, 2, 3)}
    right, left, opp = (pipe, row, (x + 1) % 4), (pipe, row, (x + 3) % 4), (pipe, row, (x + 2) % 4)
    nxt, prv = ((pipe + 1) % 8, row, x), ((pipe + 7) % 8, row, x)

    dest = ((x + 2) % 4, (x + 1) % 4, (x + 3) % 4, x)

    wcopies = []
    for rel in range(4):
        d = dest[rel]
        full = pl.multiple_of(448 * d + 64 * (d % 2), 128)
        half = pl.multiple_of(384 + 896 * (d // 2), 128)
        parts = (
            (gate_hbm, full, 384, 0), (up_hbm, full, 384, 384),
            (gate_hbm, half, 128, 768), (up_hbm, half, 128, 896),
        )
        group = []
        for i, (src, off, width, at) in enumerate(parts):
            cp = pltpu.make_async_copy(
                src.at[:, pl.ds(off, width)], w.at[rel, :, pl.ds(at, width)], w_sem.at[4 * rel + i]
            )
            cp.start()
            group.append(cp)
        wcopies.append(group)
    par = x % 2
    dcopies = [
        pltpu.make_async_copy(
            down_hbm.at[pl.ds(pl.multiple_of(64 * par, 64), 384), :], wd.at[pl.ds(0, 384), :], w_sem.at[16]
        ),
        pltpu.make_async_copy(
            down_hbm.at[pl.ds(pl.multiple_of(384 * (1 - par), 64), 64), :], wd.at[pl.ds(384, 64), :], w_sem.at[17]
        ),
    ]
    for cp in dcopies:
        cp.start()

    barrier = pltpu.get_barrier_semaphore()
    peers = (partner, zpeer[1], zpeer[2], zpeer[3], right, left, opp, nxt, prv)
    for peer in peers:
        pl.semaphore_signal(barrier, inc=1, device_id=peer, device_id_type=MESH)

    wd[448:512, :] = jnp.zeros((64, 4096), BF16)
    xs[0, 0:32, :] = tok_ref[...]

    pl.semaphore_wait(barrier, len(peers))

    sends = []

    def send(kind, e, src, dst, device):
        i = e * NK + KINDS.index(kind)
        cp = pltpu.make_async_remote_copy(
            src_ref=src, dst_ref=dst, send_sem=send_sem.at[i], recv_sem=recv_sem.at[i],
            device_id=device, device_id_type=MESH,
        )
        cp.start()
        sends.append(cp)
        return cp

    msg = {}

    def go(kind, e, src, dst, device):
        msg[kind, e] = send(kind, e, src, dst, device)

    def arrived(kind, e):
        msg[kind, e].wait_recv()

    go("fwd", 0, tok_ref, xs.at[0, pl.ds(32, 32), :], partner)
    for e in ORDER[1:]:
        go("tok", e, tok_ref, xs.at[e, pl.ds(0, 32), :], zpeer[e])

    diagonal = lax.broadcasted_iota(jnp.int32, (64, 128), 0) == lax.broadcasted_iota(jnp.int32, (64, 128), 1)
    low_half = lax.broadcasted_iota(jnp.int32, (64, 128), 1) < 64
    weights_here = [False] * 4

    def gates(e):
        if e:
            arrived("tok", e)
            go("fwd", e, xs.at[e, pl.ds(0, 32), :], xs.at[e, pl.ds(32, 32), :], partner)
        arrived("fwd", e)
        raw = xs[e].astype(F32)
        lhs = (raw * gain_ref[...]).astype(BF16)
        square = jnp.sum(raw * raw, axis=1, keepdims=True)
        compact = jnp.sum(jnp.where(diagonal, square, 0.0), axis=0, keepdims=True)
        for rel in range(4):
            if not weights_here[rel]:
                for cp in wcopies[rel]:
                    cp.wait()
                weights_here[rel] = True
            flip = (dest[rel] % 2) * 64
            for n in range(4):
                y = jnp.dot(lhs, w[rel, :, 256 * n : 256 * n + 256], preferred_element_type=F32)
                if n == 3:
                    y = jnp.where(
                        low_half,
                        pltpu.roll(y[:, 0:128], flip, 1),
                        pltpu.roll(y[:, 128:256], 64 - flip, 1),
                    )
                c = slice(256 * n, 256 * n + y.shape[1])
                if rel == OPP:
                    p1[e, :, c] = y.astype(BF16)
                elif rel == RIGHT:
                    d3[e, 0, :, c] = y[0:32].astype(BF16)
                    q[e, 0, :, c] = y[32:64]
                elif rel == LEFT:
                    d3[e, 1, :, c] = y[32:64].astype(BF16)
                    q[e, 1, :, c] = y[0:32]
                else:
                    own[e, :, c] = y
            if rel == OPP:
                go("m1r", e, p1.at[e, pl.ds(32, 32), :], r1.at[e, 0], right)
                go("m1l", e, p1.at[e, pl.ds(0, 32), :], r1.at[e, 1], left)
            elif rel == RIGHT:
                go("m3r", e, d3.at[e, 0], r3.at[e, 0], right)
            elif rel == LEFT:
                go("m3l", e, d3.at[e, 1], r3.at[e, 1], left)
                ssend[e] = jnp.broadcast_to(compact, (8, 128))
                go("ss_r", e, ssend.at[e], srecv.at[e, 0], right)
                go("ss_l", e, ssend.at[e], srecv.at[e, 1], left)
                go("ss_o", e, ssend.at[e], srecv.at[e, 2], opp)

    def relay(e):
        for kind, i, device in (("r", 0, right), ("l", 1, left)):
            arrived("m1" + kind, e)
            m2[e, i] = (q[e, i] + r1[e, i].astype(F32)).astype(BF16)
            go("m2" + kind, e, m2.at[e, i], r2.at[e, i], device)

    down_here = [False]

    def downs(e):
        for kind in ("ss_r", "ss_l", "ss_o", "m3r", "m3l", "m2r", "m2l"):
            arrived(kind, e)
        total = ssend[e] + srecv[e, 0] + srecv[e, 1] + srecv[e, 2]
        column = jnp.sum(
            jnp.where(diagonal, jnp.broadcast_to(total[0:1], (64, 128)), 0.0), axis=1, keepdims=True
        )
        inverse = lax.rsqrt(column / D + EPS)
        for half in range(2):
            rows = slice(32 * half, 32 * half + 32)
            inv = inverse[rows]
            a, b = (r3[e, 0], r2[e, 1]) if half == 0 else (r2[e, 0], r3[e, 1])
            v = (own[e, rows, :] + a.astype(F32) + b.astype(F32)) * inv
            g, u, m = v[:, 0:384], v[:, 384:768], v[:, 768:896]
            hid[rows, 0:384] = (g / (1.0 + jnp.exp(-g)) * u).astype(BF16)
            hm = m / (1.0 + jnp.exp(-m)) * pltpu.roll(m, 64, 1)
            hid[rows, 384:512] = jnp.where(low_half[0:32], hm, 0.0).astype(BF16)
        if not down_here[0]:
            for cp in dcopies:
                cp.wait()
            down_here[0] = True
        h = hid[...]
        for rel in range(4):
            for n in range(4):
                cols = pl.ds(pl.multiple_of(dest[rel] * 1024 + 256 * n, 256), 256)
                y = jnp.dot(h, wd[:, cols], preferred_element_type=F32)
                c = slice(256 * n, 256 * n + 256)
                ps[e, rel, :, c] = y[32:64].astype(BF16)
                po[e, rel, :, c] = y[0:32]
            go(f"ex{rel}", e, ps.at[e, rel], pr.at[e, rel], partner)

    def spread(e):
        for rel in range(4):
            arrived(f"ex{rel}", e)
            s = po[e, rel] + pr[e, rel].astype(F32)
            if rel == OPP:
                n1[e] = s.astype(BF16)
                go("n1r", e, n1.at[e, pl.ds(16, 16), :], t1.at[e, 0], right)
                go("n1l", e, n1.at[e, pl.ds(0, 16), :], t1.at[e, 1], left)
            elif rel == RIGHT:
                n3[e, 0] = s[0:16].astype(BF16)
                nq[e, 0] = s[16:32]
                go("n3r", e, n3.at[e, 0], t3.at[e, 0], right)
            elif rel == LEFT:
                n3[e, 1] = s[16:32].astype(BF16)
                nq[e, 1] = s[0:16]
                go("n3l", e, n3.at[e, 1], t3.at[e, 1], left)
            else:
                racc[e] = s

    def spread_relay(e):
        for kind, i, device in (("r", 0, right), ("l", 1, left)):
            arrived("n1" + kind, e)
            n2[e, i] = (nq[e, i] + t1[e, i].astype(F32)).astype(BF16)
            go("n2" + kind, e, n2.at[e, i], t2.at[e, i], device)

    def collect(e):
        for kind in ("n3r", "n3l", "n2r", "n2l"):
            arrived(kind, e)
        top = racc[e, 0:16] + t3[e, 0].astype(F32) + t2[e, 1].astype(F32)
        bottom = racc[e, 16:32] + t2[e, 0].astype(F32) + t3[e, 1].astype(F32)
        if e == 0:
            racc[e, 0:16] = top
            racc[e, 16:32] = bottom
        else:
            zsend[e, 0:16] = top.astype(BF16)
            zsend[e, 16:32] = bottom.astype(BF16)
            go("zr", e, zsend.at[e], zrecv.at[e], zpeer[e])

    e0, e1, e2, e3 = ORDER
    gates(e0)
    gates(e1)
    relay(e0)
    gates(e2)
    relay(e1)
    downs(e0)
    gates(e3)
    relay(e2)
    downs(e1)
    relay(e3)
    spread(e0)
    spread(e1)
    downs(e2)
    spread_relay(e0)
    spread(e2)
    spread_relay(e1)
    collect(e0)
    downs(e3)
    spread_relay(e2)
    collect(e1)
    spread(e3)
    collect(e2)
    spread_relay(e3)
    collect(e3)

    for e in ORDER[1:]:
        arrived("zr", e)
    branch = racc[0] + zrecv[1].astype(F32) + zrecv[2].astype(F32) + zrecv[3].astype(F32)
    hsend[...] = (tok_ref[...].astype(F32) + branch.astype(BF16).astype(F32)).astype(BF16)
    go("hand", 0, hsend, out_ref, nxt)
    arrived("hand", 0)
    for cp in sends:
        cp.wait_send()


def local(tokens, norm_gain, gate_weight, up_weight, down_weight):
    v = pltpu.VMEM
    handed = pl.pallas_call(
        kernel,
        out_shape=jax.ShapeDtypeStruct((32, 1024), BF16),
        in_specs=[pl.BlockSpec(memory_space=pltpu.VMEM)] * 2 + [pl.BlockSpec(memory_space=pl.ANY)] * 3,
        out_specs=pl.BlockSpec(memory_space=pltpu.VMEM),
        scratch_shapes=[
            v((4, 1024, 1024), BF16), v((512, 4096), BF16), v((4, 64, 1024), BF16),
            v((4, 8, 128), F32), v((4, 3, 8, 128), F32),
            v((4, 64, 896), BF16), v((4, 2, 32, 896), BF16), v((4, 2, 32, 896), F32),
            v((4, 2, 32, 896), BF16), v((4, 64, 896), F32),
            v((4, 2, 32, 896), BF16), v((4, 2, 32, 896), BF16), v((4, 2, 32, 896), BF16),
            v((64, 512), BF16), v((4, 4, 32, 1024), BF16), v((4, 4, 32, 1024), BF16), v((4, 4, 32, 1024), F32),
            v((4, 32, 1024), BF16), v((4, 2, 16, 1024), BF16), v((4, 2, 16, 1024), BF16), v((4, 2, 16, 1024), F32),
            v((4, 2, 16, 1024), BF16), v((4, 2, 16, 1024), BF16), v((4, 2, 16, 1024), BF16),
            v((4, 32, 1024), F32), v((4, 32, 1024), BF16), v((4, 32, 1024), BF16), v((32, 1024), BF16),
            pltpu.SemaphoreType.DMA((4 * NK,)), pltpu.SemaphoreType.DMA((4 * NK,)), pltpu.SemaphoreType.DMA((18,)),
        ],
        compiler_params=pltpu.CompilerParams(collective_id=0, has_side_effects=True),
        name="section",
    )(tokens[0], norm_gain, gate_weight[0], up_weight[0], down_weight[0])
    return handed[None]


def solution(mesh):
    placed = (
        P("pipe", "row", "col"),
        P("pipe", "col"),
        P("pipe", "col", "row"),
        P("pipe", "col", "row"),
        P("pipe", ("row", "col"), None),
    )
    return jax.shard_map(
        local, mesh=mesh, in_specs=placed, out_specs=P("pipe", "row", "col"), check_vma=False
    )
```

```python
import functools

import jax
import jax.numpy as jnp
from jax import lax
from jax.experimental import pallas as pl
from jax.experimental.pallas import tpu as pltpu
from jax.sharding import PartitionSpec as P

D = 4096
EPS = 1e-05
MESH = pl.DeviceIdType.MESH
F32 = jnp.float32
BF16 = jnp.bfloat16

ORDER = (0, 1, 2, 3)
OPP, RIGHT, LEFT, OWN = 0, 1, 2, 3

KINDS = (
    "tok", "fwd", "ss_r", "ss_l", "ss_o",
    "m1r", "m1l", "m3r", "m3l", "m2r", "m2l",
    "ex0", "ex1", "ex2", "ex3",
    "n1r", "n1l", "n3r", "n3l", "n2r", "n2l",
    "piece", "pass",
)
NK = len(KINDS)


def kernel(
    tok_hbm, gain_hbm, gate_hbm, up_hbm, down_hbm, out_ref,
    gain_ref, w, wd, xs, ssend, srecv,
    p1, d3, q, m2, own, r1, r3, r2,
    hid, ps, pr, po, n1, n3, n2, nq, t1, t3, t2,
    racc, psend,
    send_sem, recv_sem, w_sem,
):
    pipe, row, x = lax.axis_index("pipe"), lax.axis_index("row"), lax.axis_index("col")
    z, core = row // 2, row % 2
    zx = {1: z + 1 - 2 * (z % 2), 2: z + 2 - 4 * (z // 2), 3: 3 - z}

    partner = (pipe, 2 * z + 1 - core, x)
    zpeer = {e: (pipe, 2 * zx[e] + core, x) for e in (1, 2, 3)}
    right, left, opp = (pipe, row, (x + 1) % 4), (pipe, row, (x + 3) % 4), (pipe, row, (x + 2) % 4)
    after, before = (pipe + 1) % 8, (pipe + 7) % 8
    nxt = {0: (after, row, x)} | {e: (after, 2 * zx[e] + core, x) for e in (1, 2, 3)}
    prv = {0: (before, row, x)} | {e: (before, 2 * zx[e] + core, x) for e in (1, 2, 3)}

    dest = ((x + 2) % 4, (x + 1) % 4, (x + 3) % 4, x)

    barrier = pltpu.get_barrier_semaphore()
    peers = (partner, *zpeer.values(), right, left, opp, *nxt.values(), *prv.values())
    for peer in peers:
        pl.semaphore_signal(barrier, inc=1, device_id=peer, device_id_type=MESH)

    first = [
        pltpu.make_async_copy(tok_hbm, xs.at[0, pl.ds(0, 32), :], w_sem.at[18]),
        pltpu.make_async_copy(gain_hbm, gain_ref, w_sem.at[19]),
    ]
    for cp in first:
        cp.start()

    wcopies = []
    for rel in range(4):
        d = dest[rel]
        full = pl.multiple_of(448 * d + 64 * (d % 2), 128)
        half = pl.multiple_of(384 + 896 * (d // 2), 128)
        parts = (
            (gate_hbm, full, 384, 0), (up_hbm, full, 384, 384),
            (gate_hbm, half, 128, 768), (up_hbm, half, 128, 896),
        )
        group = []
        for i, (src, off, width, at) in enumerate(parts):
            cp = pltpu.make_async_copy(
                src.at[:, pl.ds(off, width)], w.at[rel, :, pl.ds(at, width)], w_sem.at[4 * rel + i]
            )
            cp.start()
            group.append(cp)
        wcopies.append(group)
    par = x % 2
    dcopies = [
        pltpu.make_async_copy(
            down_hbm.at[pl.ds(pl.multiple_of(64 * par, 64), 384), :], wd.at[pl.ds(0, 384), :], w_sem.at[16]
        ),
        pltpu.make_async_copy(
            down_hbm.at[pl.ds(pl.multiple_of(384 * (1 - par), 64), 64), :], wd.at[pl.ds(384, 64), :], w_sem.at[17]
        ),
    ]
    for cp in dcopies:
        cp.start()

    wd[448:512, :] = jnp.zeros((64, 4096), BF16)

    pl.semaphore_wait(barrier, len(peers))

    sends = []

    def send(kind, e, src, dst, device):
        i = e * NK + KINDS.index(kind)
        cp = pltpu.make_async_remote_copy(
            src_ref=src, dst_ref=dst, send_sem=send_sem.at[i], recv_sem=recv_sem.at[i],
            device_id=device, device_id_type=MESH,
        )
        cp.start()
        sends.append(cp)
        return cp

    msg = {}

    def go(kind, e, src, dst, device):
        msg[kind, e] = send(kind, e, src, dst, device)

    def arrived(kind, e):
        msg[kind, e].wait_recv()

    go("fwd", 0, tok_hbm, xs.at[0, pl.ds(32, 32), :], partner)
    for e in ORDER[1:]:
        go("tok", e, tok_hbm, xs.at[e, pl.ds(0, 32), :], zpeer[e])
    for cp in first:
        cp.wait()

    diagonal = lax.broadcasted_iota(jnp.int32, (64, 128), 0) == lax.broadcasted_iota(jnp.int32, (64, 128), 1)
    low_half = lax.broadcasted_iota(jnp.int32, (64, 128), 1) < 64
    weights_here = [False] * 4

    def forward(e):
        arrived("tok", e)
        go("fwd", e, xs.at[e, pl.ds(0, 32), :], xs.at[e, pl.ds(32, 32), :], partner)

    def gates(e):
        arrived("fwd", e)
        raw = xs[e].astype(F32)
        lhs = (raw * gain_ref[...]).astype(BF16)
        square = jnp.sum(raw * raw, axis=1, keepdims=True)
        compact = jnp.sum(jnp.where(diagonal, square, 0.0), axis=0, keepdims=True)
        for rel in range(4):
            if not weights_here[rel]:
                for cp in wcopies[rel]:
                    cp.wait()
                weights_here[rel] = True
            flip = (dest[rel] % 2) * 64
            for n in range(4):
                y = jnp.dot(lhs, w[rel, :, 256 * n : 256 * n + 256], preferred_element_type=F32)
                if n == 3:
                    y = jnp.where(
                        low_half,
                        pltpu.roll(y[:, 0:128], flip, 1),
                        pltpu.roll(y[:, 128:256], 64 - flip, 1),
                    )
                c = slice(256 * n, 256 * n + y.shape[1])
                if rel == OPP:
                    p1[e, :, c] = y.astype(BF16)
                elif rel == RIGHT:
                    d3[e, 0, :, c] = y[0:32].astype(BF16)
                    q[e, 0, :, c] = y[32:64]
                elif rel == LEFT:
                    d3[e, 1, :, c] = y[32:64].astype(BF16)
                    q[e, 1, :, c] = y[0:32]
                else:
                    own[e, :, c] = y
            if rel == OPP:
                go("m1r", e, p1.at[e, pl.ds(32, 32), :], r1.at[e, 0], right)
                go("m1l", e, p1.at[e, pl.ds(0, 32), :], r1.at[e, 1], left)
            elif rel == RIGHT:
                go("m3r", e, d3.at[e, 0], r3.at[e, 0], right)
            elif rel == LEFT:
                go("m3l", e, d3.at[e, 1], r3.at[e, 1], left)
                ssend[e] = jnp.broadcast_to(compact, (8, 128))
                go("ss_r", e, ssend.at[e], srecv.at[e, 0], right)
                go("ss_l", e, ssend.at[e], srecv.at[e, 1], left)
                go("ss_o", e, ssend.at[e], srecv.at[e, 2], opp)

    def relay(e):
        for kind, i, device in (("r", 0, right), ("l", 1, left)):
            arrived("m1" + kind, e)
            m2[e, i] = (q[e, i] + r1[e, i].astype(F32)).astype(BF16)
            go("m2" + kind, e, m2.at[e, i], r2.at[e, i], device)

    down_here = [False]

    def downs(e):
        for kind in ("ss_r", "ss_l", "ss_o", "m3r", "m3l", "m2r", "m2l"):
            arrived(kind, e)
        total = ssend[e] + srecv[e, 0] + srecv[e, 1] + srecv[e, 2]
        column = jnp.sum(
            jnp.where(diagonal, jnp.broadcast_to(total[0:1], (64, 128)), 0.0), axis=1, keepdims=True
        )
        inverse = lax.rsqrt(column / D + EPS)
        for half in range(2):
            rows = slice(32 * half, 32 * half + 32)
            inv = inverse[rows]
            a, b = (r3[e, 0], r2[e, 1]) if half == 0 else (r2[e, 0], r3[e, 1])
            v = (own[e, rows, :] + a.astype(F32) + b.astype(F32)) * inv
            g, u, m = v[:, 0:384], v[:, 384:768], v[:, 768:896]
            hid[rows, 0:384] = (g / (1.0 + jnp.exp(-g)) * u).astype(BF16)
            hm = m / (1.0 + jnp.exp(-m)) * pltpu.roll(m, 64, 1)
            hid[rows, 384:512] = jnp.where(low_half[0:32], hm, 0.0).astype(BF16)
        if not down_here[0]:
            for cp in dcopies:
                cp.wait()
            down_here[0] = True
        h = hid[...]
        for rel in range(4):
            for n in range(4):
                cols = pl.ds(pl.multiple_of(dest[rel] * 1024 + 256 * n, 256), 256)
                y = jnp.dot(h, wd[:, cols], preferred_element_type=F32)
                c = slice(256 * n, 256 * n + 256)
                ps[e, rel, :, c] = y[32:64].astype(BF16)
                po[e, rel, :, c] = y[0:32]
            go(f"ex{rel}", e, ps.at[e, rel], pr.at[e, rel], partner)

    def spread(e):
        for rel in range(4):
            arrived(f"ex{rel}", e)
            s = po[e, rel] + pr[e, rel].astype(F32)
            if rel == OPP:
                n1[e] = s.astype(BF16)
                go("n1r", e, n1.at[e, pl.ds(16, 16), :], t1.at[e, 0], right)
                go("n1l", e, n1.at[e, pl.ds(0, 16), :], t1.at[e, 1], left)
            elif rel == RIGHT:
                n3[e, 0] = s[0:16].astype(BF16)
                nq[e, 0] = s[16:32]
                go("n3r", e, n3.at[e, 0], t3.at[e, 0], right)
            elif rel == LEFT:
                n3[e, 1] = s[16:32].astype(BF16)
                nq[e, 1] = s[0:16]
                go("n3l", e, n3.at[e, 1], t3.at[e, 1], left)
            else:
                racc[e] = s

    def spread_relay(e):
        for kind, i, device in (("r", 0, right), ("l", 1, left)):
            arrived("n1" + kind, e)
            n2[e, i] = (nq[e, i] + t1[e, i].astype(F32)).astype(BF16)
            go("n2" + kind, e, n2.at[e, i], t2.at[e, i], device)

    def collect(e):
        for kind in ("n3r", "n3l", "n2r", "n2l"):
            arrived(kind, e)
        top = racc[e, 0:16] + t3[e, 0].astype(F32) + t2[e, 1].astype(F32)
        bottom = racc[e, 16:32] + t2[e, 0].astype(F32) + t3[e, 1].astype(F32)
        psend[e, 0:16] = top.astype(BF16)
        psend[e, 16:32] = bottom.astype(BF16)
        go("piece", e, psend.at[e], out_ref.at[e], nxt[e])

    e0, e1, e2, e3 = ORDER
    gates(e0)
    forward(e1)
    gates(e1)
    forward(e2)
    relay(e0)
    gates(e2)
    forward(e3)
    relay(e1)
    gates(e3)
    go("pass", 0, tok_hbm, out_ref.at[4], nxt[0])
    relay(e2)
    downs(e0)
    downs(e1)
    relay(e3)
    spread(e0)
    spread(e1)
    downs(e2)
    spread_relay(e0)
    downs(e3)
    spread(e2)
    spread_relay(e1)
    collect(e0)
    spread(e3)
    spread_relay(e2)
    collect(e1)
    spread_relay(e3)
    collect(e2)
    collect(e3)

    arrived("pass", 0)
    for e in ORDER:
        arrived("piece", e)
    for cp in sends:
        cp.wait_send()


def local(tokens, norm_gain, gate_weight, up_weight, down_weight):
    v = pltpu.VMEM
    pieces = pl.pallas_call(
        kernel,
        out_shape=pltpu.VMEM((5, 32, 1024), BF16),
        in_specs=[pl.BlockSpec(memory_space=pl.ANY)] * 5,
        out_specs=pl.BlockSpec(memory_space=pltpu.VMEM),
        scratch_shapes=[
            v((1, 1024), F32), v((4, 1024, 1024), BF16), v((512, 4096), BF16), v((4, 64, 1024), BF16),
            v((4, 8, 128), F32), v((4, 3, 8, 128), F32),
            v((4, 64, 896), BF16), v((4, 2, 32, 896), BF16), v((4, 2, 32, 896), F32),
            v((4, 2, 32, 896), BF16), v((4, 64, 896), F32),
            v((4, 2, 32, 896), BF16), v((4, 2, 32, 896), BF16), v((4, 2, 32, 896), BF16),
            v((64, 512), BF16), v((4, 4, 32, 1024), BF16), v((4, 4, 32, 1024), BF16), v((4, 4, 32, 1024), F32),
            v((4, 32, 1024), BF16), v((4, 2, 16, 1024), BF16), v((4, 2, 16, 1024), BF16), v((4, 2, 16, 1024), F32),
            v((4, 2, 16, 1024), BF16), v((4, 2, 16, 1024), BF16), v((4, 2, 16, 1024), BF16),
            v((4, 32, 1024), F32), v((4, 32, 1024), BF16),
            pltpu.SemaphoreType.DMA((4 * NK,)), pltpu.SemaphoreType.DMA((4 * NK,)), pltpu.SemaphoreType.DMA((20,)),
        ],
        compiler_params=pltpu.CompilerParams(collective_id=0, has_side_effects=True),
        name="section",
    )(tokens[0], norm_gain, gate_weight[0], up_weight[0], down_weight[0])
    parts = [pieces[e].astype(F32) for e in range(5)]
    branch = (parts[0] + parts[1] + parts[2] + parts[3]).astype(BF16)
    return (parts[4] + branch.astype(F32)).astype(BF16)[None]


def solution(mesh):
    placed = (
        P("pipe", "row", "col"),
        P("pipe", "col"),
        P("pipe", "col", "row"),
        P("pipe", "col", "row"),
        P("pipe", ("row", "col"), None),
    )
    return jax.shard_map(
        local, mesh=mesh, in_specs=placed, out_specs=P("pipe", "row", "col"), check_vma=False
    )
```

```python
import functools

import jax
import jax.numpy as jnp
from jax import lax
from jax.experimental import pallas as pl
from jax.experimental.pallas import tpu as pltpu
from jax.sharding import PartitionSpec as P

D = 4096
EPS = 1e-05
MESH = pl.DeviceIdType.MESH
F32 = jnp.float32
BF16 = jnp.bfloat16

SLOT = {0: 0, 2: 1, 3: 2}
OPP, RIGHT, LEFT, OWN = 0, 1, 2, 3

KINDS = (
    "tok", "fwd", "ss_r", "ss_l", "ss_o",
    "m1r", "m1l", "m3r", "m3l", "m2r", "m2l",
    "ex0", "ex1", "ex2", "ex3",
    "n1r", "n1l", "n3r", "n3l", "n2r", "n2l",
    "piece", "zf0", "zf1", "zf2", "zf3",
)
NK = len(KINDS)


def kernel(
    tok_hbm, gain_hbm, gate_hbm, up_hbm, down_hbm, out_ref,
    gain_ref, w, wd, xs, ssend, srecv,
    p1, d3, q, m2, own, r1, r3, r2,
    hid, ps, pr, po, n1, n3, n2, nq, t1, t3, t2,
    racc, psend, zs, zr,
    send_sem, recv_sem, w_sem,
):
    pipe, row, x = lax.axis_index("pipe"), lax.axis_index("row"), lax.axis_index("col")
    z, core = row // 2, row % 2
    zx = {0: z, 1: z + 1 - 2 * (z % 2), 2: z + 2 - 4 * (z // 2), 3: 3 - z}

    partner = (pipe, 2 * z + 1 - core, x)
    zpeer = {e: (pipe, 2 * zx[e] + core, x) for e in (1, 2, 3)}
    right, left, opp = (pipe, row, (x + 1) % 4), (pipe, row, (x + 3) % 4), (pipe, row, (x + 2) % 4)
    after, before = (pipe + 1) % 8, (pipe + 7) % 8
    nxt = {e: (after, 2 * zx[e] + core, x) for e in SLOT}
    prv = {e: (before, 2 * zx[e] + core, x) for e in SLOT}

    dest = ((x + 2) % 4, (x + 1) % 4, (x + 3) % 4, x)

    barrier = pltpu.get_barrier_semaphore()
    peers = (partner, *zpeer.values(), right, left, opp, *nxt.values(), *prv.values())
    for peer in peers:
        pl.semaphore_signal(barrier, inc=1, device_id=peer, device_id_type=MESH)

    first = [
        pltpu.make_async_copy(tok_hbm, xs.at[0, pl.ds(0, 32), :], w_sem.at[18]),
        pltpu.make_async_copy(gain_hbm, gain_ref, w_sem.at[19]),
    ]
    for cp in first:
        cp.start()

    wcopies = []
    for rel in range(4):
        d = dest[rel]
        full = pl.multiple_of(448 * d + 64 * (d % 2), 128)
        half = pl.multiple_of(384 + 896 * (d // 2), 128)
        parts = (
            (gate_hbm, full, 384, 0), (up_hbm, full, 384, 384),
            (gate_hbm, half, 128, 768), (up_hbm, half, 128, 896),
        )
        group = []
        for i, (src, off, width, at) in enumerate(parts):
            cp = pltpu.make_async_copy(
                src.at[:, pl.ds(off, width)], w.at[rel, :, pl.ds(at, width)], w_sem.at[4 * rel + i]
            )
            group.append(cp)
        wcopies.append(group)
    par = x % 2
    dcopies = [
        pltpu.make_async_copy(
            down_hbm.at[pl.ds(pl.multiple_of(64 * par, 64), 384), :], wd.at[pl.ds(0, 384), :], w_sem.at[16]
        ),
        pltpu.make_async_copy(
            down_hbm.at[pl.ds(pl.multiple_of(384 * (1 - par), 64), 64), :], wd.at[pl.ds(384, 64), :], w_sem.at[17]
        ),
    ]

    def start(copies):
        for cp in copies:
            cp.start()

    start(wcopies[OPP])
    start(wcopies[RIGHT])
    wd[448:512, :] = jnp.zeros((64, 4096), BF16)

    sends = []

    def send(kind, e, src, dst, device):
        i = e * NK + KINDS.index(kind)
        cp = pltpu.make_async_remote_copy(
            src_ref=src, dst_ref=dst, send_sem=send_sem.at[i], recv_sem=recv_sem.at[i],
            device_id=device, device_id_type=MESH,
        )
        cp.start()
        sends.append(cp)
        return cp

    msg = {}

    def go(kind, e, src, dst, device):
        msg[kind, e] = send(kind, e, src, dst, device)

    def arrived(kind, e):
        msg[kind, e].wait_recv()

    diagonal = lax.broadcasted_iota(jnp.int32, (64, 128), 0) == lax.broadcasted_iota(jnp.int32, (64, 128), 1)
    low_half = lax.broadcasted_iota(jnp.int32, (64, 128), 1) < 64
    weights_here = [False] * 4
    def forward(e):
        arrived("tok", e)
        go("fwd", e, xs.at[e, pl.ds(0, 32), :], xs.at[e, pl.ds(32, 32), :], partner)

    def scaled(es, half="ab"):
        lo, hi = {"a": (0, 32), "b": (32, 64), "ab": (0, 64)}[half]
        rows = [(xs[e, lo:hi, :].astype(F32) * gain_ref[...]).astype(BF16) for e in es]
        return rows[0] if len(rows) == 1 else jnp.concatenate(rows, axis=0)

    def product(es, rel, lhs, half="ab"):
        if not weights_here[rel]:
            for cp in wcopies[rel]:
                cp.wait()
            weights_here[rel] = True
        flip = (dest[rel] % 2) * 64
        lo, hi = {"a": (0, 32), "b": (32, 64), "ab": (0, 64)}[half]
        for n in range(4):
            block = jnp.dot(lhs, w[rel, :, 256 * n : 256 * n + 256], preferred_element_type=F32)
            for i, e in enumerate(es):
                y = block[(hi - lo) * i : (hi - lo) * (i + 1)]
                if n == 3:
                    y = jnp.where(
                        low_half[0 : hi - lo],
                        pltpu.roll(y[:, 0:128], flip, 1),
                        pltpu.roll(y[:, 128:256], 64 - flip, 1),
                    )
                c = slice(256 * n, 256 * n + y.shape[1])
                if rel == OPP:
                    p1[e, lo:hi, c] = y.astype(BF16)
                elif rel == OWN:
                    own[e, lo:hi, c] = y
                else:
                    if "a" in half:
                        if rel == RIGHT:
                            d3[e, 0, :, c] = y[0:32].astype(BF16)
                        else:
                            q[e, 1, :, c] = y[0:32]
                    if "b" in half:
                        if rel == RIGHT:
                            q[e, 0, :, c] = y[-32:]
                        else:
                            d3[e, 1, :, c] = y[-32:].astype(BF16)
        for e in es:
            if rel == OPP and "b" in half:
                go("m1r", e, p1.at[e, pl.ds(32, 32), :], r1.at[e, 0], right)
            if rel == OPP and "a" in half and (e or half != "a"):
                go("m1l", e, p1.at[e, pl.ds(0, 32), :], r1.at[e, 1], left)
            if rel == RIGHT and half == "ab":
                go("m3r", e, d3.at[e, 0], r3.at[e, 0], right)
            if rel == LEFT and "b" in half:
                go("m3l", e, d3.at[e, 1], r3.at[e, 1], left)

    def squares(e):
        raw = xs[e].astype(F32)
        square = jnp.sum(raw * raw, axis=1, keepdims=True)
        compact = jnp.sum(jnp.where(diagonal, square, 0.0), axis=0, keepdims=True)
        ssend[e] = jnp.broadcast_to(compact, (8, 128))
        go("ss_r", e, ssend.at[e], srecv.at[e, 0], right)
        go("ss_l", e, ssend.at[e], srecv.at[e, 1], left)
        go("ss_o", e, ssend.at[e], srecv.at[e, 2], opp)

    def relay(e, ways="rl"):
        for kind, i, device in (("r", 0, right), ("l", 1, left)):
            if kind in ways:
                arrived("m1" + kind, e)
                m2[e, i] = (q[e, i] + r1[e, i].astype(F32)).astype(BF16)
                go("m2" + kind, e, m2.at[e, i], r2.at[e, i], device)

    down_here = [False]

    def hiddens(e, at):
        for kind in ("ss_r", "ss_l", "ss_o", "m3r", "m3l", "m2r", "m2l"):
            arrived(kind, e)
        total = ssend[e] + srecv[e, 0] + srecv[e, 1] + srecv[e, 2]
        column = jnp.sum(
            jnp.where(diagonal, jnp.broadcast_to(total[0:1], (64, 128)), 0.0), axis=1, keepdims=True
        )
        inverse = lax.rsqrt(column / D + EPS)
        for half in range(2):
            rows = slice(32 * half, 32 * half + 32)
            put = slice(64 * at + 32 * half, 64 * at + 32 * half + 32)
            inv = inverse[rows]
            a, b = (r3[e, 0], r2[e, 1]) if half == 0 else (r2[e, 0], r3[e, 1])
            v = (own[e, rows, :] + a.astype(F32) + b.astype(F32)) * inv
            g, u, m = v[:, 0:384], v[:, 384:768], v[:, 768:896]
            hid[put, 0:384] = (g / (1.0 + jnp.exp(-g)) * u).astype(BF16)
            hm = m / (1.0 + jnp.exp(-m)) * pltpu.roll(m, 64, 1)
            hid[put, 384:512] = jnp.where(low_half[0:32], hm, 0.0).astype(BF16)

    def downs(*es, at=0, between=()):
        if not down_here[0]:
            for cp in dcopies:
                cp.wait()
            down_here[0] = True
        h = hid[64 * at : 64 * (at + len(es)), :]
        for rel in range(4):
            for n in range(4):
                cols = pl.ds(pl.multiple_of(dest[rel] * 1024 + 256 * n, 256), 256)
                y = jnp.dot(h, wd[:, cols], preferred_element_type=F32)
                c = slice(256 * n, 256 * n + 256)
                for i, e in enumerate(es):
                    ps[e, rel, :, c] = y[64 * i + 32 : 64 * i + 64].astype(BF16)
                    po[e, rel, :, c] = y[64 * i : 64 * i + 32]
            for e in es:
                go(f"ex{rel}", e, ps.at[e, rel], pr.at[e, rel], partner)
            if rel < len(between):
                between[rel]()

    def rows_first(e):
        for rel in range(4):
            arrived(f"ex{rel}", e)
            zs[rel] = (po[e, rel] + pr[e, rel].astype(F32)).astype(BF16)
            go(f"zf{rel}", e, zs.at[rel], zr.at[rel], zpeer[e])

    def spread(e, rels=(OPP, RIGHT, LEFT, OWN)):
        for rel in rels:
            arrived(f"ex{rel}", e)
            s = po[e, rel] + pr[e, rel].astype(F32)
            if e == 0:
                arrived(f"zf{rel}", 1)
                s = s + zr[rel].astype(F32)
            if rel == OPP:
                n1[e] = s.astype(BF16)
                go("n1r", e, n1.at[e, pl.ds(16, 16), :], t1.at[e, 0], right)
                go("n1l", e, n1.at[e, pl.ds(0, 16), :], t1.at[e, 1], left)
            elif rel == RIGHT:
                n3[e, 0] = s[0:16].astype(BF16)
                nq[e, 0] = s[16:32]
                go("n3r", e, n3.at[e, 0], t3.at[e, 0], right)
            elif rel == LEFT:
                n3[e, 1] = s[16:32].astype(BF16)
                nq[e, 1] = s[0:16]
                go("n3l", e, n3.at[e, 1], t3.at[e, 1], left)
            else:
                racc[e] = s

    def spread_relay(e):
        for kind, i, device in (("r", 0, right), ("l", 1, left)):
            arrived("n1" + kind, e)
            n2[e, i] = (nq[e, i] + t1[e, i].astype(F32)).astype(BF16)
            go("n2" + kind, e, n2.at[e, i], t2.at[e, i], device)

    def collect(e):
        for kind in ("n3r", "n3l", "n2r", "n2l"):
            arrived(kind, e)
        top = racc[e, 0:16] + t3[e, 0].astype(F32) + t2[e, 1].astype(F32)
        bottom = racc[e, 16:32] + t2[e, 0].astype(F32) + t3[e, 1].astype(F32)
        if e == 0:
            top = top + xs[0, 0:16, :].astype(F32)
            bottom = bottom + xs[0, 16:32, :].astype(F32)
        psend[e, 0:16] = top.astype(BF16)
        psend[e, 16:32] = bottom.astype(BF16)
        go("piece", e, psend.at[e], out_ref.at[SLOT[e]], nxt[e])

    for cp in first:
        cp.wait()
    lhs = scaled((0,), "a")
    product((0,), OPP, lhs, "a")
    start(wcopies[LEFT])
    product((0,), RIGHT, lhs, "a")
    start(wcopies[OWN])

    pl.semaphore_wait(barrier, len(peers))

    mine = xs.at[0, pl.ds(0, 32), :]
    go("fwd", 0, mine, xs.at[0, pl.ds(32, 32), :], partner)
    go("tok", 1, mine, xs.at[1, pl.ds(0, 32), :], zpeer[1])
    go("m1l", 0, p1.at[0, pl.ds(0, 32), :], r1.at[0, 1], left)
    go("m3r", 0, d3.at[0, 0], r3.at[0, 0], right)
    start(dcopies)
    arrived("fwd", 0)
    for e in (2, 3):
        go("tok", e, mine, xs.at[e, pl.ds(0, 32), :], zpeer[e])
    lhs = scaled((0,), "b")
    product((0,), OPP, lhs, "b")
    product((0,), LEFT, scaled((0,)))
    product((0,), RIGHT, lhs, "b")
    forward(1)
    squares(0)
    relay(0, "l")
    arrived("fwd", 1)
    lhs = scaled((1,))
    product((1,), OPP, lhs)
    product((1,), RIGHT, lhs)
    product((1,), LEFT, lhs)
    forward(2)
    relay(0, "r")
    product((0, 1), OWN, scaled((0, 1)))
    squares(1)
    forward(3)
    relay(1)
    arrived("fwd", 2)
    arrived("fwd", 3)
    lhs = scaled((2, 3))
    product((2, 3), OPP, lhs)
    product((2, 3), RIGHT, lhs)
    product((2, 3), LEFT, lhs)
    hiddens(0, 0)
    hiddens(1, 1)
    downs(0, 1)
    squares(2)
    squares(3)
    relay(2)
    rows_first(1)
    relay(3)
    product((2, 3), OWN, lhs)
    spread(0, (OPP,))
    hiddens(2, 0)
    downs(2)
    spread(0, (RIGHT,))
    hiddens(3, 1)
    spread(0, (LEFT,))
    spread_relay(0)
    downs(
        3,
        at=1,
        between=(
            lambda: spread(2, (OPP,)),
            lambda: spread(2, (RIGHT,)),
            lambda: spread(2, (LEFT,)),
        ),
    )
    spread(3, (OPP,))
    spread(0, (OWN,))
    spread(2, (OWN,))
    spread(3, (RIGHT, LEFT, OWN))
    collect(0)
    spread_relay(2)
    spread_relay(3)
    collect(2)
    collect(3)

    for e in SLOT:
        arrived("piece", e)
    for cp in sends:
        cp.wait_send()


def local(tokens, norm_gain, gate_weight, up_weight, down_weight):
    v = pltpu.VMEM
    pieces = pl.pallas_call(
        kernel,
        out_shape=pltpu.VMEM((3, 32, 1024), BF16),
        in_specs=[pl.BlockSpec(memory_space=pl.ANY)] * 5,
        out_specs=pl.BlockSpec(memory_space=pltpu.VMEM),
        scratch_shapes=[
            v((1, 1024), F32), v((4, 1024, 1024), BF16), v((512, 4096), BF16), v((4, 64, 1024), BF16),
            v((4, 8, 128), F32), v((4, 3, 8, 128), F32),
            v((4, 64, 896), BF16), v((4, 2, 32, 896), BF16), v((4, 2, 32, 896), F32),
            v((4, 2, 32, 896), BF16), v((4, 64, 896), F32),
            v((4, 2, 32, 896), BF16), v((4, 2, 32, 896), BF16), v((4, 2, 32, 896), BF16),
            v((128, 512), BF16), v((4, 4, 32, 1024), BF16), v((4, 4, 32, 1024), BF16), v((4, 4, 32, 1024), F32),
            v((4, 32, 1024), BF16), v((4, 2, 16, 1024), BF16), v((4, 2, 16, 1024), BF16), v((4, 2, 16, 1024), F32),
            v((4, 2, 16, 1024), BF16), v((4, 2, 16, 1024), BF16), v((4, 2, 16, 1024), BF16),
            v((4, 32, 1024), F32), v((4, 32, 1024), BF16), v((4, 32, 1024), BF16), v((4, 32, 1024), BF16),
            pltpu.SemaphoreType.DMA((4 * NK,)), pltpu.SemaphoreType.DMA((4 * NK,)), pltpu.SemaphoreType.DMA((20,)),
        ],
        compiler_params=pltpu.CompilerParams(collective_id=0, has_side_effects=True),
        name="section",
    )(tokens[0], norm_gain, gate_weight[0], up_weight[0], down_weight[0])
    first, second, third = (pieces[i].astype(F32) for i in range(3))
    return (first + (second + third)).astype(BF16)[None]


def solution(mesh):
    placed = (
        P("pipe", "row", "col"),
        P("pipe", "col"),
        P("pipe", "col", "row"),
        P("pipe", "col", "row"),
        P("pipe", ("row", "col"), None),
    )
    return jax.shard_map(
        local, mesh=mesh, in_specs=placed, out_specs=P("pipe", "row", "col"), check_vma=False
    )
```

```python
import functools

import jax
import jax.numpy as jnp
from jax import lax
from jax.experimental import pallas as pl
from jax.experimental.pallas import tpu as pltpu
from jax.sharding import PartitionSpec as P

D = 4096
EPS = 1e-05
MESH = pl.DeviceIdType.MESH
F32 = jnp.float32
BF16 = jnp.bfloat16

SLOT = {0: 0, 2: 1, 3: 2}
OPP, RIGHT, LEFT, OWN = 0, 1, 2, 3

KINDS = (
    "tok", "fwd", "ss_r", "ss_l", "ss_o",
    "m1r", "m1l", "m3r", "m3l", "m2r", "m2l",
    "ex0", "ex1", "ex2", "ex3",
    "n1r", "n1l", "n3r", "n3l", "n2r", "n2l",
    "piece", "zf0", "zf1", "zf2", "zf3",
)
NK = len(KINDS)


def kernel(
    tok_hbm, gain_hbm, gate_hbm, up_hbm, down_hbm, out_ref,
    gain_ref, w, wd, xs, ssend, srecv,
    p1, d3, q, m2, own, r1, r3, r2,
    hid, ps, pr, po, n1, n3, n2, nq, t1, t3, t2,
    racc, psend, zs, zr,
    send_sem, recv_sem, w_sem,
):
    pipe, row, x = lax.axis_index("pipe"), lax.axis_index("row"), lax.axis_index("col")
    z, core = row // 2, row % 2
    zx = {0: z, 1: z + 1 - 2 * (z % 2), 2: z + 2 - 4 * (z // 2), 3: 3 - z}

    partner = (pipe, 2 * z + 1 - core, x)
    zpeer = {e: (pipe, 2 * zx[e] + core, x) for e in (1, 2, 3)}
    right, left, opp = (pipe, row, (x + 1) % 4), (pipe, row, (x + 3) % 4), (pipe, row, (x + 2) % 4)
    after, before = (pipe + 1) % 8, (pipe + 7) % 8
    nxt = {e: (after, 2 * zx[e] + core, x) for e in SLOT}
    prv = {e: (before, 2 * zx[e] + core, x) for e in SLOT}

    dest = ((x + 2) % 4, (x + 1) % 4, (x + 3) % 4, x)

    barrier = pltpu.get_barrier_semaphore()
    peers = (partner, *zpeer.values(), right, left, opp, *nxt.values(), *prv.values())
    for peer in peers:
        pl.semaphore_signal(barrier, inc=1, device_id=peer, device_id_type=MESH)

    first = [
        pltpu.make_async_copy(tok_hbm, xs.at[0, pl.ds(0, 32), :], w_sem.at[18]),
        pltpu.make_async_copy(gain_hbm, gain_ref, w_sem.at[19]),
    ]
    for cp in first:
        cp.start()

    wcopies = []
    for rel in range(4):
        d = dest[rel]
        full = pl.multiple_of(448 * d + 64 * (d % 2), 128)
        half = pl.multiple_of(384 + 896 * (d // 2), 128)
        parts = (
            (gate_hbm, full, 384, 0), (up_hbm, full, 384, 384),
            (gate_hbm, half, 128, 768), (up_hbm, half, 128, 896),
        )
        group = []
        for i, (src, off, width, at) in enumerate(parts):
            cp = pltpu.make_async_copy(
                src.at[:, pl.ds(off, width)], w.at[rel, :, pl.ds(at, width)], w_sem.at[4 * rel + i]
            )
            group.append(cp)
        wcopies.append(group)
    par = x % 2
    dcopies = [
        pltpu.make_async_copy(
            down_hbm.at[pl.ds(pl.multiple_of(64 * par, 64), 384), :], wd.at[pl.ds(0, 384), :], w_sem.at[16]
        ),
        pltpu.make_async_copy(
            down_hbm.at[pl.ds(pl.multiple_of(384 * (1 - par), 64), 64), :], wd.at[pl.ds(384, 64), :], w_sem.at[17]
        ),
    ]

    def start(copies):
        for cp in copies:
            cp.start()

    start(wcopies[OPP])
    start(wcopies[RIGHT])
    wd[448:512, :] = jnp.zeros((64, 4096), BF16)

    sends = []

    def send(kind, e, src, dst, device):
        i = e * NK + KINDS.index(kind)
        cp = pltpu.make_async_remote_copy(
            src_ref=src, dst_ref=dst, send_sem=send_sem.at[i], recv_sem=recv_sem.at[i],
            device_id=device, device_id_type=MESH,
        )
        cp.start()
        sends.append(cp)
        return cp

    msg = {}

    def go(kind, e, src, dst, device):
        msg[kind, e] = send(kind, e, src, dst, device)

    def arrived(kind, e):
        msg[kind, e].wait_recv()

    diagonal = lax.broadcasted_iota(jnp.int32, (64, 128), 0) == lax.broadcasted_iota(jnp.int32, (64, 128), 1)
    low_half = lax.broadcasted_iota(jnp.int32, (64, 128), 1) < 64
    weights_here = [False] * 4
    def forward(e):
        arrived("tok", e)
        go("fwd", e, xs.at[e, pl.ds(0, 32), :], xs.at[e, pl.ds(32, 32), :], partner)

    def scaled(es, half="ab"):
        lo, hi = {"a": (0, 32), "b": (32, 64), "ab": (0, 64)}[half]
        rows = [(xs[e, lo:hi, :].astype(F32) * gain_ref[...]).astype(BF16) for e in es]
        return rows[0] if len(rows) == 1 else jnp.concatenate(rows, axis=0)

    def product(es, rel, lhs, half="ab"):
        if not weights_here[rel]:
            for cp in wcopies[rel]:
                cp.wait()
            weights_here[rel] = True
        flip = (dest[rel] % 2) * 64
        lo, hi = {"a": (0, 32), "b": (32, 64), "ab": (0, 64)}[half]
        for n in range(4):
            block = jnp.dot(lhs, w[rel, :, 256 * n : 256 * n + 256], preferred_element_type=F32)
            for i, e in enumerate(es):
                y = block[(hi - lo) * i : (hi - lo) * (i + 1)]
                if n == 3:
                    y = jnp.where(
                        low_half[0 : hi - lo],
                        pltpu.roll(y[:, 0:128], flip, 1),
                        pltpu.roll(y[:, 128:256], 64 - flip, 1),
                    )
                c = slice(256 * n, 256 * n + y.shape[1])
                if rel == OPP:
                    p1[e, lo:hi, c] = y.astype(BF16)
                elif rel == OWN:
                    own[e, lo:hi, c] = y
                else:
                    if "a" in half:
                        if rel == RIGHT:
                            d3[e, 0, :, c] = y[0:32].astype(BF16)
                        else:
                            q[e, 1, :, c] = y[0:32]
                    if "b" in half:
                        if rel == RIGHT:
                            q[e, 0, :, c] = y[-32:]
                        else:
                            d3[e, 1, :, c] = y[-32:].astype(BF16)
        for e in es:
            if rel == OPP and "b" in half:
                go("m1r", e, p1.at[e, pl.ds(32, 32), :], r1.at[e, 0], right)
            if rel == OPP and "a" in half and (e or half != "a"):
                go("m1l", e, p1.at[e, pl.ds(0, 32), :], r1.at[e, 1], left)
            if rel == RIGHT and half == "ab":
                go("m3r", e, d3.at[e, 0], r3.at[e, 0], right)
            if rel == LEFT and "b" in half:
                go("m3l", e, d3.at[e, 1], r3.at[e, 1], left)

    def squares(e):
        raw = xs[e].astype(F32)
        square = jnp.sum(raw * raw, axis=1, keepdims=True)
        compact = jnp.sum(jnp.where(diagonal, square, 0.0), axis=0, keepdims=True)
        ssend[e] = jnp.broadcast_to(compact, (8, 128))
        go("ss_r", e, ssend.at[e], srecv.at[e, 0], right)
        go("ss_l", e, ssend.at[e], srecv.at[e, 1], left)
        go("ss_o", e, ssend.at[e], srecv.at[e, 2], opp)

    def relay(e, ways="rl"):
        for kind, i, device in (("r", 0, right), ("l", 1, left)):
            if kind in ways:
                arrived("m1" + kind, e)
                m2[e, i] = (q[e, i] + r1[e, i].astype(F32)).astype(BF16)
                go("m2" + kind, e, m2.at[e, i], r2.at[e, i], device)

    down_here = [False]

    def hiddens(e, at):
        for kind in ("ss_r", "ss_l", "ss_o", "m3r", "m3l", "m2r", "m2l"):
            arrived(kind, e)
        total = ssend[e] + srecv[e, 0] + srecv[e, 1] + srecv[e, 2]
        column = jnp.sum(
            jnp.where(diagonal, jnp.broadcast_to(total[0:1], (64, 128)), 0.0), axis=1, keepdims=True
        )
        inverse = lax.rsqrt(column / D + EPS)
        for half in range(2):
            rows = slice(32 * half, 32 * half + 32)
            put = slice(64 * at + 32 * half, 64 * at + 32 * half + 32)
            inv = inverse[rows]
            a, b = (r3[e, 0], r2[e, 1]) if half == 0 else (r2[e, 0], r3[e, 1])
            v = (own[e, rows, :] + a.astype(F32) + b.astype(F32)) * inv
            g, u, m = v[:, 0:384], v[:, 384:768], v[:, 768:896]
            hid[put, 0:384] = (g / (1.0 + jnp.exp(-g)) * u).astype(BF16)
            hm = m / (1.0 + jnp.exp(-m)) * pltpu.roll(m, 64, 1)
            hid[put, 384:512] = jnp.where(low_half[0:32], hm, 0.0).astype(BF16)

    def downs(*es, at=0, between=()):
        if not down_here[0]:
            for cp in dcopies:
                cp.wait()
            down_here[0] = True
        h = hid[64 * at : 64 * (at + len(es)), :]
        for rel in range(4):
            for n in range(4):
                cols = pl.ds(pl.multiple_of(dest[rel] * 1024 + 256 * n, 256), 256)
                y = jnp.dot(h, wd[:, cols], preferred_element_type=F32)
                c = slice(256 * n, 256 * n + 256)
                for i, e in enumerate(es):
                    ps[e, rel, :, c] = y[64 * i + 32 : 64 * i + 64].astype(BF16)
                    po[e, rel, :, c] = y[64 * i : 64 * i + 32]
            for e in es:
                go(f"ex{rel}", e, ps.at[e, rel], pr.at[e, rel], partner)
            if rel < len(between):
                between[rel]()

    def rows_first(e):
        for rel in range(4):
            arrived(f"ex{rel}", e)
            zs[rel] = (po[e, rel] + pr[e, rel].astype(F32)).astype(BF16)
            go(f"zf{rel}", e, zs.at[rel], zr.at[rel], zpeer[e])

    def spread(e, rels=(OPP, RIGHT, LEFT, OWN)):
        for rel in rels:
            arrived(f"ex{rel}", e)
            s = po[e, rel] + pr[e, rel].astype(F32)
            if e == 0:
                arrived(f"zf{rel}", 1)
                s = s + zr[rel].astype(F32)
            if rel == OPP:
                n1[e] = s.astype(BF16)
                go("n1r", e, n1.at[e, pl.ds(16, 16), :], t1.at[e, 0], right)
                go("n1l", e, n1.at[e, pl.ds(0, 16), :], t1.at[e, 1], left)
            elif rel == RIGHT:
                n3[e, 0] = s[0:16].astype(BF16)
                nq[e, 0] = s[16:32]
                go("n3r", e, n3.at[e, 0], t3.at[e, 0], right)
            elif rel == LEFT:
                n3[e, 1] = s[16:32].astype(BF16)
                nq[e, 1] = s[0:16]
                go("n3l", e, n3.at[e, 1], t3.at[e, 1], left)
            else:
                racc[e] = s

    def spread_relay(e):
        for kind, i, device in (("r", 0, right), ("l", 1, left)):
            arrived("n1" + kind, e)
            n2[e, i] = (nq[e, i] + t1[e, i].astype(F32)).astype(BF16)
            go("n2" + kind, e, n2.at[e, i], t2.at[e, i], device)

    def collect(e):
        for kind in ("n3r", "n3l", "n2r", "n2l"):
            arrived(kind, e)
        top = racc[e, 0:16] + t3[e, 0].astype(F32) + t2[e, 1].astype(F32)
        bottom = racc[e, 16:32] + t2[e, 0].astype(F32) + t3[e, 1].astype(F32)
        if e == 0:
            top = top + xs[0, 0:16, :].astype(F32)
            bottom = bottom + xs[0, 16:32, :].astype(F32)
        psend[e, 0:16] = top.astype(BF16)
        psend[e, 16:32] = bottom.astype(BF16)
        go("piece", e, psend.at[e], out_ref.at[SLOT[e]], nxt[e])

    for cp in first:
        cp.wait()
    lhs = scaled((0,), "a")
    product((0,), OPP, lhs, "a")
    start(wcopies[LEFT])
    product((0,), RIGHT, lhs, "a")
    start(wcopies[OWN])

    pl.semaphore_wait(barrier, len(peers))

    mine = xs.at[0, pl.ds(0, 32), :]
    go("fwd", 0, mine, xs.at[0, pl.ds(32, 32), :], partner)
    go("tok", 1, mine, xs.at[1, pl.ds(0, 32), :], zpeer[1])
    go("m1l", 0, p1.at[0, pl.ds(0, 32), :], r1.at[0, 1], left)
    go("m3r", 0, d3.at[0, 0], r3.at[0, 0], right)
    start(dcopies)
    arrived("fwd", 0)
    go("tok", 2, mine, xs.at[2, pl.ds(0, 32), :], zpeer[2])
    lhs = scaled((0,), "b")
    product((0,), OPP, lhs, "b")
    product((0,), LEFT, scaled((0,)))
    product((0,), RIGHT, lhs, "b")
    forward(1)
    go("tok", 3, mine, xs.at[3, pl.ds(0, 32), :], zpeer[3])
    squares(0)
    relay(0, "l")
    arrived("fwd", 1)
    lhs = scaled((1,))
    product((1,), OPP, lhs)
    product((1,), RIGHT, lhs)
    product((1,), LEFT, lhs)
    forward(2)
    relay(0, "r")
    product((0, 1), OWN, scaled((0, 1)))
    arrived("fwd", 2)
    lhs = scaled((2,))
    product((2,), OPP, lhs)
    forward(3)
    squares(1)
    relay(1)
    product((2,), RIGHT, lhs)
    product((2,), LEFT, lhs)
    arrived("fwd", 3)
    lhs = scaled((3,))
    product((3,), OPP, lhs)
    product((3,), RIGHT, lhs)
    product((3,), LEFT, lhs)
    squares(2)
    hiddens(0, 0)
    hiddens(1, 1)
    downs(0, 1)
    relay(2)
    squares(3)
    rows_first(1)
    relay(3)
    product((2, 3), OWN, scaled((2, 3)))
    spread(0, (OPP,))
    hiddens(2, 0)
    downs(2)
    spread(0, (RIGHT,))
    hiddens(3, 1)
    spread(0, (LEFT,))
    spread_relay(0)
    downs(
        3,
        at=1,
        between=(
            lambda: spread(2, (OPP,)),
            lambda: spread(2, (RIGHT,)),
            lambda: spread(2, (LEFT,)),
        ),
    )
    spread(3, (OPP,))
    spread(0, (OWN,))
    spread(2, (OWN,))
    spread(3, (RIGHT, LEFT, OWN))
    collect(0)
    spread_relay(2)
    spread_relay(3)
    collect(2)
    collect(3)

    for e in SLOT:
        arrived("piece", e)
    for cp in sends:
        cp.wait_send()


def local(tokens, norm_gain, gate_weight, up_weight, down_weight):
    v = pltpu.VMEM
    pieces = pl.pallas_call(
        kernel,
        out_shape=pltpu.VMEM((3, 32, 1024), BF16),
        in_specs=[pl.BlockSpec(memory_space=pl.ANY)] * 5,
        out_specs=pl.BlockSpec(memory_space=pltpu.VMEM),
        scratch_shapes=[
            v((1, 1024), F32), v((4, 1024, 1024), BF16), v((512, 4096), BF16), v((4, 64, 1024), BF16),
            v((4, 8, 128), F32), v((4, 3, 8, 128), F32),
            v((4, 64, 896), BF16), v((4, 2, 32, 896), BF16), v((4, 2, 32, 896), F32),
            v((4, 2, 32, 896), BF16), v((4, 64, 896), F32),
            v((4, 2, 32, 896), BF16), v((4, 2, 32, 896), BF16), v((4, 2, 32, 896), BF16),
            v((128, 512), BF16), v((4, 4, 32, 1024), BF16), v((4, 4, 32, 1024), BF16), v((4, 4, 32, 1024), F32),
            v((4, 32, 1024), BF16), v((4, 2, 16, 1024), BF16), v((4, 2, 16, 1024), BF16), v((4, 2, 16, 1024), F32),
            v((4, 2, 16, 1024), BF16), v((4, 2, 16, 1024), BF16), v((4, 2, 16, 1024), BF16),
            v((4, 32, 1024), F32), v((4, 32, 1024), BF16), v((4, 32, 1024), BF16), v((4, 32, 1024), BF16),
            pltpu.SemaphoreType.DMA((4 * NK,)), pltpu.SemaphoreType.DMA((4 * NK,)), pltpu.SemaphoreType.DMA((20,)),
        ],
        compiler_params=pltpu.CompilerParams(collective_id=0, has_side_effects=True),
        name="section",
    )(tokens[0], norm_gain, gate_weight[0], up_weight[0], down_weight[0])
    first, second, third = (pieces[i].astype(F32) for i in range(3))
    return (first + (second + third)).astype(BF16)[None]


def solution(mesh):
    placed = (
        P("pipe", "row", "col"),
        P("pipe", "col"),
        P("pipe", "col", "row"),
        P("pipe", "col", "row"),
        P("pipe", ("row", "col"), None),
    )
    return jax.shard_map(
        local, mesh=mesh, in_specs=placed, out_specs=P("pipe", "row", "col"), check_vma=False
    )
```
